32 devices in a mesh: rep: 2 (over x), ga: 16 (over z, y, core).
Axes of the slice: x: 2, y: 2, z: 4, core: 2. Of those that a mesh axis runs over, the one named last changes fastest.
Arguments:
- positions: float32 [64, 3, 768], P('rep', None, 'ga'), parts along dimension 0, may hold values from -3 to 23, as said below
- weights: int32 [1, 32], replicated, may hold values from 1 to 16
- psi: bfloat16 [2, 512, 2, 32768], P('rep', None, None, 'ga'), parts along dimension 0, may hold values from -5 to 5
- vloc: float32 [2, 32768], P('rep'), parts along dimension 0, may hold values from -8 to 8
Outputs:
- psi_new: bfloat16 [2, 512, 2, 32768], P('rep', None, None, 'ga'), parts along dimension 0
- bead_forces: float32 [64, 3, 768], P('rep', None, 'ga'), parts along dimension 0
The draws below stay inside these ranges and needn't reach their ends.
There are 2 independent parts, one for each index of `rep`. The reference program is written for one: setup_inputs(seed, part) draws one part's arguments, and reference() takes and returns one part's arrays. A program takes and returns all parts, laid end to end along the dimension named above; an argument that names none is the same for every part. Nothing has to cross between parts.
Inputs may be any that keep to these rules, and one draw needn't show every extreme that they name: `positions`: atom 3w is the oxygen of water w and atoms 3w+1 and 3w+2 are its hydrogens; in every bead each hydrogen lies between 1.0 and 2.6 from its oxygen.
All inputs are finite; a program needn't handle non-finite values.
Results may differ from the reference program's by a relative error of at most 0.0037.
The reference program's roundings to bfloat16 on the way (of `table`, `projections`, `trial` and `mixer`) count: a program that leaves them out, or rounds other values in their place, can miss the bound.
Values may be sent and summed in bfloat16 or wider, within the bound.
A program may use at most 192 MiB of HBM per device.

```python
import jax
import jax.numpy as jnp
from jax import lax

BEADS = 32
CBEADS = 1
WATERS = 256
ATOMS = 768
BANDS = 512
NGRID = 32
GVECS = 32768


def draw_positions(key, part):
    subkeys = jax.random.split(jax.random.fold_in(key, 7), 5)
    oxygen = jax.random.uniform(subkeys[0], (3, WATERS), jnp.float32, 0.0, 20.0)
    first_dir = jax.random.normal(subkeys[1], (3, WATERS), jnp.float32)
    second_dir = jax.random.normal(subkeys[2], (3, WATERS), jnp.float32)
    first_dir = first_dir / jnp.sqrt(jnp.sum(first_dir * first_dir, axis=0, keepdims=True) + 1e-06)
    second_dir = second_dir / jnp.sqrt(jnp.sum(second_dir * second_dir, axis=0, keepdims=True) + 1e-06)
    lengths = jax.random.uniform(subkeys[3], (2, WATERS), jnp.float32, 1.5, 2.1)
    centroid = jnp.stack([oxygen, oxygen + lengths[0] * first_dir, oxygen + lengths[1] * second_dir], axis=2).reshape(3, ATOMS)
    spread = jax.random.uniform(subkeys[4], (BEADS, 3, ATOMS), jnp.float32, -0.12, 0.12)
    return centroid[None] + spread


def with_ends(array, stream_key, least, top_value):
    spot = [jax.random.randint(jax.random.fold_in(stream_key, axis), (), 0, length) for axis, length in enumerate(array.shape)]
    longest = array.shape.index(max(array.shape))
    next_to = spot[:longest] + [(spot[longest] + 1) % array.shape[longest]] + spot[longest + 1:]
    return array.at[tuple(spot)].set(least).at[tuple(next_to)].set(top_value)


def block_scale(rng, dims, pieces, low, top_value):
    loudness, own = 1.0, jax.random.fold_in(rng, 6)
    for axis_at, parts in pieces:
        steps = jnp.exp(jax.random.uniform(jax.random.fold_in(own, axis_at), (parts,), jnp.float32, low / len(pieces), top_value / len(pieces)))
        loudness = loudness * jnp.repeat(steps, dims[axis_at] // parts).reshape([-1 if axis == axis_at else 1 for axis in range(len(dims))])
    return loudness


def bell_draw(stream_key, extent, scale, most, shards=(), kind=jnp.bfloat16):
    entries = jax.random.normal(stream_key, extent, jnp.float32) * scale
    if len(shards) > 0:
        entries = block_scale(stream_key, extent, shards, -0.22, 0.18) * entries
    return jnp.clip(entries, min=-most, max=most).astype(kind)


def setup_inputs(seed: int = 0, part: int = 0) -> dict:
    streams_of = jax.random.split(jax.random.key(seed), 5)
    part_splits = jax.random.split(jax.random.fold_in(streams_of[4], part), 5)
    positions = draw_positions(jax.random.fold_in(jax.random.fold_in(streams_of[4], part), 71), part)
    weights = with_ends(jax.random.randint(streams_of[1], (CBEADS, BEADS), 1, 17), jax.random.fold_in(streams_of[1], 1), 1, 16).astype(jnp.int32)
    psi = bell_draw(part_splits[2], (CBEADS, BANDS, 2, GVECS), 0.7071, 5.0, ((3, 16),))
    vloc = jnp.clip(jax.random.uniform(part_splits[3], (CBEADS, GVECS), jnp.float32, -8.0, 8.0), -8.0, 8.0)
    return {"positions": positions, "weights": weights, "psi": psi, "vloc": vloc}


box_length = 20.0
bond_stiff = 0.5
bond_rest = 1.8
spring_stiff = 2.0
width_square = 0.09
step_size = 0.02
nonlocal_strength = 250.0
occupation = 2.0
highest = lax.Precision.HIGHEST

def frequency(index, count):
    signed = jnp.where(index < count // 2, index, index - count)
    return signed.astype(jnp.float32) * (2.0 * jnp.pi / box_length)

def field_forces(positions):
    oxygen = positions[:, :, 0::3]
    toward_one = positions[:, :, 1::3] - oxygen
    toward_two = positions[:, :, 2::3] - oxygen

    def stretch(offset):
        length = jnp.sqrt(lax.optimization_barrier(jnp.sum(offset * offset, axis=1, keepdims=True)))
        return -bond_stiff * (length - bond_rest) * offset / length
    pull_one = stretch(toward_one)
    pull_two = stretch(toward_two)
    bonds = jnp.stack([-(pull_one + pull_two), pull_one, pull_two], axis=3).reshape(positions.shape)
    springs = 2.0 * positions - jnp.roll(positions, 1, axis=0) - jnp.roll(positions, -1, axis=0)
    return bonds - spring_stiff * springs

def inner(left_mat, right_mat):
    return lax.dot_general(left_mat, right_mat, (((1,), (1,)), ((), ())), preferred_element_type=jnp.float32)

def reference(positions, weights, psi, vloc):
    near_forces = field_forces(positions)
    weight_float = weights.astype(jnp.float32)
    mixing = weight_float / lax.optimization_barrier(jnp.sum(weight_float, axis=1, keepdims=True))
    centres = jnp.einsum('cj,jan->can', mixing, positions, precision=highest)
    flat_index = jnp.arange(GVECS, dtype=jnp.int32)
    gvectors = jnp.stack([frequency(flat_index // (NGRID * NGRID), NGRID), frequency(flat_index // NGRID % NGRID, NGRID), frequency(flat_index % NGRID, NGRID)])
    square = lax.optimization_barrier(jnp.sum(gvectors * gvectors, axis=0))
    profile = jnp.exp(-0.5 * width_square * square)
    kinetic = 0.5 * square
    new_waves = []
    dft_forces = []
    for contracted in range(CBEADS):
        oxygens = centres[contracted][:, 0::3]
        phases = jnp.einsum('ai,ag->ig', oxygens, gvectors, precision=highest)
        wave_cos = profile * jnp.cos(phases)
        wave_sin = profile * jnp.sin(phases)
        table = jnp.concatenate([jnp.concatenate([wave_cos, -wave_sin], 1), jnp.concatenate([wave_sin, wave_cos], 1)], 0).astype(jnp.bfloat16)
        wavefunc = psi[contracted].reshape(BANDS, 2 * GVECS)
        real_part = wavefunc[:, :GVECS]
        imag_part = wavefunc[:, GVECS:]
        projections = (inner(table, wavefunc) * (1.0 / GVECS)).astype(jnp.bfloat16)
        nonlocal_term = lax.dot_general(projections, table, (((0,), (0,)), ((), ())), preferred_element_type=jnp.float32)
        paired = jnp.concatenate([wavefunc, jnp.concatenate([imag_part, -real_part], 1)], 0)
        side_by_side = jnp.concatenate([projections[:WATERS], projections[WATERS:]], 1)
        weighted = jnp.dot(side_by_side, paired, preferred_element_type=jnp.float32)
        mixed_wave = wave_cos * weighted[:, GVECS:] + wave_sin * weighted[:, :GVECS]
        oxygen_force = 2.0 * occupation * nonlocal_strength / GVECS * jnp.einsum('ag,ig->ai', gvectors, mixed_wave, precision=highest)
        hydrogen_zero = jnp.zeros_like(oxygen_force)
        dft_forces.append(jnp.stack([oxygen_force, hydrogen_zero, hydrogen_zero], axis=2).reshape(3, ATOMS))
        grid_potential = vloc[contracted].reshape(NGRID, NGRID, NGRID)

        def apply_block(band_block):
            complex_wave = (band_block[:, 0].astype(jnp.float32) + 1j * band_block[:, 1].astype(jnp.float32)).reshape(-1, NGRID, NGRID, NGRID)
            spread = jnp.fft.fftn(grid_potential * jnp.fft.ifftn(complex_wave, axes=(1, 2, 3)), axes=(1, 2, 3)).reshape(-1, GVECS)
            return jnp.stack([jnp.real(spread), jnp.imag(spread)], axis=1).astype(jnp.float32)
        blocks = min(64, BANDS)
        potential_term = lax.map(apply_block, psi[contracted].reshape(BANDS // blocks, blocks, 2, GVECS)).reshape(BANDS, 2, GVECS)
        wave_float = psi[contracted].astype(jnp.float32)
        hamil_re = kinetic * wave_float[:, 0] + potential_term[:, 0] + nonlocal_strength * nonlocal_term[:, :GVECS]
        hamil_im = kinetic * wave_float[:, 1] + potential_term[:, 1] + nonlocal_strength * nonlocal_term[:, GVECS:]
        trial = jnp.concatenate([wave_float[:, 0] - step_size * hamil_re, wave_float[:, 1] - step_size * hamil_im], 1).astype(jnp.bfloat16)
        rotated = jnp.concatenate([trial, jnp.concatenate([-trial[:, GVECS:], trial[:, :GVECS]], 1)], 0)
        margin = inner(trial, rotated) * (1.0 / GVECS)
        identity_rows = jnp.concatenate([jnp.eye(BANDS, dtype=jnp.float32), jnp.zeros((BANDS, BANDS), jnp.float32)], 1)
        mixer = (1.5 * identity_rows - 0.5 * margin).astype(jnp.bfloat16)
        updated = jnp.dot(mixer, rotated, preferred_element_type=jnp.float32).astype(jnp.bfloat16)
        new_waves.append(updated.reshape(BANDS, 2, GVECS))
    contracted_force = jnp.einsum('cj,can->jan', mixing, jnp.stack(dft_forces), precision=highest)
    bead_forces = near_forces + BEADS / CBEADS * contracted_force
    return (jnp.stack(new_waves), bead_forces)
```

```python
import jax
import jax.numpy as jnp
import numpy as np
from jax import lax
from jax.sharding import PartitionSpec as P

BEADS = 32
CBEADS = 1
WATERS = 256
NGRID = 32
GVECS = 32768
CHUNKS = 2


box_length = 20.0
bond_stiff = 0.5
bond_rest = 1.8
spring_stiff = 2.0
width_square = 0.09
step_size = 0.02
nonlocal_strength = 250.0
occupation = 2.0
highest = lax.Precision.HIGHEST


def frequency(index, count):
    signed = jnp.where(index < count // 2, index, index - count)
    return signed.astype(jnp.float32) * (2.0 * jnp.pi / box_length)


def field_forces(positions):
    oxygen = positions[:, :, 0::3]
    toward_one = positions[:, :, 1::3] - oxygen
    toward_two = positions[:, :, 2::3] - oxygen

    def stretch(offset):
        length = jnp.sqrt(jnp.sum(offset * offset, axis=1, keepdims=True))
        return -bond_stiff * (length - bond_rest) * offset / length

    pull_one = stretch(toward_one)
    pull_two = stretch(toward_two)
    bonds = jnp.stack([-(pull_one + pull_two), pull_one, pull_two], axis=3).reshape(positions.shape)
    springs = 2.0 * positions - jnp.roll(positions, 1, axis=0) - jnp.roll(positions, -1, axis=0)
    return bonds - spring_stiff * springs


def inner(left_mat, right_mat):
    return lax.dot_general(
        left_mat, right_mat, (((1,), (1,)), ((), ())), preferred_element_type=jnp.float32
    )


def real_form(freq_index, group_index):
    product = freq_index[:, None] * freq_index[None, :] % NGRID
    angle = product.astype(jnp.float32) * (2.0 * jnp.pi / NGRID)
    same = (group_index[:, None] == group_index[None, :]).astype(jnp.float32)
    cosines = jnp.cos(angle) * same
    sines = jnp.sin(angle) * same
    return jnp.stack([jnp.stack([cosines, sines], 1), jnp.stack([-sines, cosines], 1)], 0)


def plane_table():
    index = jnp.arange(NGRID, dtype=jnp.int32)
    return real_form(index, jnp.zeros_like(index))


def block_table(length, within):
    index = jnp.arange(length, dtype=jnp.int32)
    if within:
        return real_form(index % NGRID, index // NGRID)
    return real_form(index // NGRID, index % NGRID)


def grid_sum(psi, vloc, parts):
    bands = psi.shape[1]
    local_g = psi.shape[3]
    x_table = plane_table()
    z_table = block_table(local_g, True)
    y_table = block_table(NGRID * NGRID, False)
    grid_potential = vloc[0].reshape(1, 1, NGRID, NGRID * NGRID)
    grouped_raw = psi[0].reshape(parts, bands // parts, 2, local_g)
    planes = lax.all_to_all(grouped_raw, "ga", split_axis=0, concat_axis=3, tiled=True)
    band_count = planes.shape[1]
    blocks_whole = planes.astype(jnp.float32).reshape(band_count, 2, NGRID**3 // local_g, local_g)
    along_z = jnp.einsum("mckp,cpdq->mdkq", blocks_whole, z_table, precision=highest) * (
        1.0 / NGRID
    )
    grid = along_z.reshape(band_count, 2, NGRID, NGRID * NGRID)
    grid = jnp.einsum("mcxr,cxdw->mdwr", grid, x_table, precision=highest) * (1.0 / NGRID)
    grid = jnp.einsum("mcxp,cpdq->mdxq", grid, y_table, precision=highest) * (1.0 / NGRID)
    grid = grid * grid_potential
    grid = jnp.einsum("mdxq,cpdq->mcxp", grid, y_table, precision=highest)
    grid = jnp.einsum("mdwr,cxdw->mcxr", grid, x_table, precision=highest)
    returning = grid.reshape(1, band_count, 2, NGRID**3)
    returned = lax.all_to_all(
        returning.astype(jnp.bfloat16), "ga", split_axis=3, concat_axis=0, tiled=True
    ).astype(returning.dtype)
    returned = returned.reshape(bands, 2, local_g)
    potential = jnp.einsum("bdq,cpdq->bcp", returned, z_table, precision=highest)
    return potential[:, 0], potential[:, 1]


def plane_rotation():
    small = np.arange(NGRID)
    angle = small[:, None] * small[None, :] % NGRID * (2.0 * np.pi / NGRID)
    side = NGRID * NGRID
    wave = np.kron(np.exp(1j * angle), np.exp(1j * angle))
    real, imag = np.real(wave), np.imag(wave)
    table = np.stack([np.stack([real, -imag], 1), np.stack([imag, real], 1)], 1)
    return jnp.asarray(table.reshape(2 * side, 2 * side).astype(np.float32), jnp.bfloat16)


def line_rotation(group):
    small = np.arange(NGRID)
    angle = small[:, None] * small[None, :] % NGRID * (2.0 * np.pi / NGRID)
    real, imag = np.cos(angle), np.sin(angle)
    form = np.stack([np.stack([real, -imag], 2), np.stack([imag, real], 2)], 1)
    same = np.eye(group)
    table = form[:, None, :, :, None, :] * same[None, :, None, None, :, None]
    size = 2 * NGRID * group
    return jnp.asarray(table.reshape(size, size).astype(np.float32), jnp.bfloat16)


def plane_sum(psi, vloc, parts):
    bands = psi.shape[1]
    local_g = psi.shape[3]
    side = NGRID * NGRID
    planes = local_g // side
    points = side // parts
    group = min(8, points)
    groups = points // group
    chunk = bands // CHUNKS
    plane_table = plane_rotation()
    line_table = line_rotation(group)
    start = lax.axis_index("ga") * points
    own = lax.dynamic_slice_in_dim(vloc[0].reshape(NGRID, side), start, points, axis=1)
    own = own.reshape(NGRID, groups, group).transpose(1, 0, 2) * (1.0 / (NGRID * side))
    own = jnp.broadcast_to(own[..., None], (groups, NGRID, group, 2)).reshape(groups, -1, 1)
    scaled = (own * line_table.astype(jnp.float32)).astype(jnp.bfloat16)
    action = jnp.einsum(
        "ea,gec->gac", line_table, scaled, preferred_element_type=jnp.float32
    ).astype(jnp.bfloat16)
    reals, imags = [], []
    for first in range(0, bands, chunk):
        part = psi[0, first : first + chunk].reshape(chunk, 2, planes, side)
        part = part.transpose(2, 0, 1, 3).reshape(planes, chunk, 2 * side)
        sent = jnp.stack(
            [
                jnp.einsum(
                    "qk,bk->qb", plane_table, part[p], preferred_element_type=jnp.float32
                )
                .astype(jnp.bfloat16)
                .reshape(parts, 2 * points, chunk)
                for p in range(planes)
            ],
            1,
        )
        lines = lax.all_to_all(sent, "ga", split_axis=0, concat_axis=0, tiled=True)
        lines = lines.reshape(parts * planes, groups, 2 * group, chunk)
        lines = lines.transpose(1, 0, 2, 3).reshape(groups, -1, chunk)
        lines = jnp.einsum(
            "gac,gcb->gab", action, lines, preferred_element_type=jnp.float32
        ).astype(jnp.bfloat16)
        lines = lines.reshape(groups, parts * planes, 2 * group, chunk).transpose(1, 0, 2, 3)
        lines = lines.reshape(parts, planes, 2 * points, chunk)
        back = lax.all_to_all(lines, "ga", split_axis=0, concat_axis=0, tiled=True)
        whole = [
            jnp.einsum(
                "qb,qk->bk",
                back[:, p].reshape(2 * side, chunk),
                plane_table,
                preferred_element_type=jnp.float32,
            )
            for p in range(planes)
        ]
        reals.append(jnp.concatenate([w[:, :side] for w in whole], 1))
        imags.append(jnp.concatenate([w[:, side:] for w in whole], 1))
    return jnp.concatenate(reals, 0), jnp.concatenate(imags, 0)


def waves(oxygens, gvectors, profile):
    local_g = profile.shape[0]
    side = NGRID * NGRID
    if local_g % side:
        phases = jnp.einsum("ai,ag->ig", oxygens, gvectors, precision=highest)
        return profile * jnp.cos(phases), profile * jnp.sin(phases)
    spots = oxygens.T
    flat = spots[:, 1:2] * gvectors[1:2, :side] + spots[:, 2:3] * gvectors[2:3, :side]
    flat_cos, flat_sin = jnp.cos(flat), jnp.sin(flat)
    along = spots[:, 0:1] * gvectors[0:1, ::side]
    along_cos, along_sin = jnp.cos(along), jnp.sin(along)
    cosines, sines = [], []
    for p in range(local_g // side):
        c, s = along_cos[:, p : p + 1], along_sin[:, p : p + 1]
        cosines.append(c * flat_cos - s * flat_sin)
        sines.append(s * flat_cos + c * flat_sin)
    return profile * jnp.concatenate(cosines, 1), profile * jnp.concatenate(sines, 1)


def per_device(positions, weights, psi, vloc):
    near_forces = field_forces(positions)
    weight_float = weights.astype(jnp.float32)
    mixing = weight_float / jnp.sum(weight_float, axis=1, keepdims=True)
    centres = jnp.einsum("cj,jan->can", mixing, positions, precision=highest)
    everyone = lax.all_gather(centres, "ga", axis=2, tiled=True)
    parts = lax.axis_size("ga")
    bands = psi.shape[1]
    local_g = psi.shape[3]
    flat_index = lax.axis_index("ga") * local_g + jnp.arange(local_g, dtype=jnp.int32)
    gvectors = jnp.stack(
        [
            frequency(flat_index // (NGRID * NGRID), NGRID),
            frequency(flat_index // NGRID % NGRID, NGRID),
            frequency(flat_index % NGRID, NGRID),
        ]
    )
    square = jnp.sum(gvectors * gvectors, axis=0)
    profile = jnp.exp(-0.5 * width_square * square)
    kinetic = 0.5 * square
    oxygens = everyone[0][:, 0::3]
    wave_cos, wave_sin = waves(oxygens, gvectors, profile)
    table = jnp.concatenate(
        [jnp.concatenate([wave_cos, -wave_sin], 1), jnp.concatenate([wave_sin, wave_cos], 1)], 0
    ).astype(jnp.bfloat16)
    wavefunc = psi[0].reshape(bands, 2 * local_g)
    real_part = wavefunc[:, :local_g]
    imag_part = wavefunc[:, local_g:]
    partial_proj = (inner(table, wavefunc) * (1.0 / GVECS)).reshape(2, WATERS, bands)
    share = lax.psum_scatter(partial_proj, "ga", scatter_dimension=1, tiled=True).astype(
        jnp.bfloat16
    )
    paired = jnp.concatenate([wavefunc, jnp.concatenate([imag_part, -real_part], 1)], 0).reshape(
        2, bands, 2 * local_g
    )
    table_blocks = table.reshape(2, WATERS, 2 * local_g)
    all_proj = lax.all_gather(share, "ga", axis=1, tiled=True)
    nonlocal_term = jnp.einsum(
        "kib,kig->bg", all_proj, table_blocks, preferred_element_type=jnp.float32
    )
    weighted = jnp.einsum("kib,kbg->ig", all_proj, paired, preferred_element_type=jnp.float32)
    mixed_wave = wave_cos * weighted[:, local_g:] + wave_sin * weighted[:, :local_g]
    force_part = (
        2.0
        * occupation
        * nonlocal_strength
        / GVECS
        * jnp.einsum("ag,ig->ai", gvectors, mixed_wave, precision=highest)
    )
    oxygen_force = lax.psum_scatter(force_part, "ga", scatter_dimension=1, tiled=True)
    hydrogen_zero = jnp.zeros_like(oxygen_force)
    dft_forces = [jnp.stack([oxygen_force, hydrogen_zero, hydrogen_zero], axis=2).reshape(3, -1)]
    wave_float = psi[0].astype(jnp.float32)
    if local_g % (NGRID * NGRID) == 0 and (NGRID * NGRID) % parts == 0:
        potential = plane_sum(psi, vloc, parts)
    else:
        potential = grid_sum(psi, vloc, parts)
    hamil_re = (
        kinetic * wave_float[:, 0]
        + potential[0]
        + nonlocal_strength * nonlocal_term[:, :local_g]
    )
    hamil_im = (
        kinetic * wave_float[:, 1]
        + potential[1]
        + nonlocal_strength * nonlocal_term[:, local_g:]
    )
    trial = jnp.concatenate(
        [wave_float[:, 0] - step_size * hamil_re, wave_float[:, 1] - step_size * hamil_im], 1
    ).astype(jnp.bfloat16)
    rotated = jnp.concatenate(
        [trial, jnp.concatenate([-trial[:, local_g:], trial[:, :local_g]], 1)], 0
    )
    row = lax.broadcasted_iota(jnp.int32, (bands, bands), 0)
    column = lax.broadcasted_iota(jnp.int32, (bands, bands), 1)
    both = inner(trial, rotated) * (1.0 / GVECS)
    packed = lax.psum(jnp.where(row <= column, both[:, :bands], both[:, bands:]), "ga")
    turned = packed.T
    even = jnp.where(row <= column, packed, turned)
    odd = jnp.where(row > column, packed, jnp.where(row < column, -turned, 0.0))
    identity = (row == column).astype(jnp.float32)
    mixer = jnp.concatenate([1.5 * identity - 0.5 * even, -0.5 * odd], 1).astype(jnp.bfloat16)
    updated = jnp.dot(mixer, rotated, preferred_element_type=jnp.float32)
    new_waves = [updated.astype(jnp.bfloat16).reshape(bands, 2, local_g)]
    contracted_force = jnp.einsum("cj,can->jan", mixing, jnp.stack(dft_forces), precision=highest)
    bead_forces = near_forces + BEADS / CBEADS * contracted_force
    return (jnp.stack(new_waves), bead_forces)


def solution(mesh):
    placed = (P("rep", None, "ga"), P(), P("rep", None, None, "ga"), P("rep", None))
    return jax.shard_map(
        per_device,
        mesh=mesh,
        in_specs=placed,
        out_specs=(P("rep", None, None, "ga"), P("rep", None, "ga")),
        check_vma=False,
    )
```

```python
import jax
import jax.numpy as jnp
import numpy as np
from jax import lax
from jax.sharding import PartitionSpec as P

BEADS = 32
CBEADS = 1
WATERS = 256
NGRID = 32
GVECS = 32768
CHUNKS = 2


box_length = 20.0
bond_stiff = 0.5
bond_rest = 1.8
spring_stiff = 2.0
width_square = 0.09
step_size = 0.02
nonlocal_strength = 250.0
occupation = 2.0
highest = lax.Precision.HIGHEST


def frequency(index, count):
    signed = jnp.where(index < count // 2, index, index - count)
    return signed.astype(jnp.float32) * (2.0 * jnp.pi / box_length)


def field_forces(positions):
    oxygen = positions[:, :, 0::3]
    toward_one = positions[:, :, 1::3] - oxygen
    toward_two = positions[:, :, 2::3] - oxygen

    def stretch(offset):
        length = jnp.sqrt(jnp.sum(offset * offset, axis=1, keepdims=True))
        return -bond_stiff * (length - bond_rest) * offset / length

    pull_one = stretch(toward_one)
    pull_two = stretch(toward_two)
    bonds = jnp.stack([-(pull_one + pull_two), pull_one, pull_two], axis=3).reshape(positions.shape)
    springs = 2.0 * positions - jnp.roll(positions, 1, axis=0) - jnp.roll(positions, -1, axis=0)
    return bonds - spring_stiff * springs


def inner(left_mat, right_mat):
    return lax.dot_general(
        left_mat, right_mat, (((1,), (1,)), ((), ())), preferred_element_type=jnp.float32
    )


def real_form(freq_index, group_index):
    product = freq_index[:, None] * freq_index[None, :] % NGRID
    angle = product.astype(jnp.float32) * (2.0 * jnp.pi / NGRID)
    same = (group_index[:, None] == group_index[None, :]).astype(jnp.float32)
    cosines = jnp.cos(angle) * same
    sines = jnp.sin(angle) * same
    return jnp.stack([jnp.stack([cosines, sines], 1), jnp.stack([-sines, cosines], 1)], 0)


def plane_table():
    index = jnp.arange(NGRID, dtype=jnp.int32)
    return real_form(index, jnp.zeros_like(index))


def block_table(length, within):
    index = jnp.arange(length, dtype=jnp.int32)
    if within:
        return real_form(index % NGRID, index // NGRID)
    return real_form(index // NGRID, index % NGRID)


def grid_sum(psi, vloc, parts):
    bands = psi.shape[1]
    local_g = psi.shape[3]
    x_table = plane_table()
    z_table = block_table(local_g, True)
    y_table = block_table(NGRID * NGRID, False)
    grid_potential = vloc[0].reshape(1, 1, NGRID, NGRID * NGRID)
    grouped_raw = psi[0].reshape(parts, bands // parts, 2, local_g)
    planes = lax.all_to_all(grouped_raw, "ga", split_axis=0, concat_axis=3, tiled=True)
    band_count = planes.shape[1]
    blocks_whole = planes.astype(jnp.float32).reshape(band_count, 2, NGRID**3 // local_g, local_g)
    along_z = jnp.einsum("mckp,cpdq->mdkq", blocks_whole, z_table, precision=highest) * (
        1.0 / NGRID
    )
    grid = along_z.reshape(band_count, 2, NGRID, NGRID * NGRID)
    grid = jnp.einsum("mcxr,cxdw->mdwr", grid, x_table, precision=highest) * (1.0 / NGRID)
    grid = jnp.einsum("mcxp,cpdq->mdxq", grid, y_table, precision=highest) * (1.0 / NGRID)
    grid = grid * grid_potential
    grid = jnp.einsum("mdxq,cpdq->mcxp", grid, y_table, precision=highest)
    grid = jnp.einsum("mdwr,cxdw->mcxr", grid, x_table, precision=highest)
    returning = grid.reshape(1, band_count, 2, NGRID**3)
    returned = lax.all_to_all(
        returning.astype(jnp.bfloat16), "ga", split_axis=3, concat_axis=0, tiled=True
    ).astype(returning.dtype)
    returned = returned.reshape(bands, 2, local_g)
    potential = jnp.einsum("bdq,cpdq->bcp", returned, z_table, precision=highest)
    return potential[:, 0], potential[:, 1]


def plane_rotation():
    small = np.arange(NGRID)
    angle = small[:, None] * small[None, :] % NGRID * (2.0 * np.pi / NGRID)
    side = NGRID * NGRID
    wave = np.kron(np.exp(1j * angle), np.exp(1j * angle))
    real, imag = np.real(wave), np.imag(wave)
    table = np.stack([np.stack([real, -imag], 1), np.stack([imag, real], 1)], 1)
    return jnp.asarray(table.reshape(2 * side, 2 * side).astype(np.float32), jnp.bfloat16)


def line_rotation(group):
    small = np.arange(NGRID)
    angle = small[:, None] * small[None, :] % NGRID * (2.0 * np.pi / NGRID)
    real, imag = np.cos(angle), np.sin(angle)
    form = np.stack([np.stack([real, -imag], 2), np.stack([imag, real], 2)], 1)
    same = np.eye(group)
    table = form[:, None, :, :, None, :] * same[None, :, None, None, :, None]
    size = 2 * NGRID * group
    return jnp.asarray(table.reshape(size, size).astype(np.float32), jnp.bfloat16)


def plane_out(psi, parts, plane_table):
    bands = psi.shape[1]
    side = NGRID * NGRID
    planes = psi.shape[3] // side
    chunk = bands // CHUNKS
    pieces = []
    for first in range(0, bands, chunk):
        part = psi[0, first : first + chunk].reshape(chunk, 2, planes, side)
        part = part.transpose(2, 0, 1, 3).reshape(planes, chunk, 2 * side)
        pieces.append(
            jnp.stack(
                [
                    jnp.einsum(
                        "qk,bk->qb", plane_table, part[p], preferred_element_type=jnp.float32
                    )
                    .astype(jnp.bfloat16)
                    .reshape(parts, 2 * side // parts, chunk)
                    for p in range(planes)
                ],
                1,
            )
        )
    return pieces


def exchange(piece):
    return lax.all_to_all(piece, "ga", split_axis=0, concat_axis=0, tiled=True)


def line_action(vloc, parts):
    side = NGRID * NGRID
    points = side // parts
    group = min(8, points)
    groups = points // group
    line_table = line_rotation(group)
    start = lax.axis_index("ga") * points
    own = lax.dynamic_slice_in_dim(vloc[0].reshape(NGRID, side), start, points, axis=1)
    own = own.reshape(NGRID, groups, group).transpose(1, 0, 2) * (1.0 / (NGRID * side))
    own = jnp.broadcast_to(own[..., None], (groups, NGRID, group, 2)).reshape(groups, -1, 1)
    scaled = (own * line_table.astype(jnp.float32)).astype(jnp.bfloat16)
    return jnp.einsum(
        "ea,gec->gac", line_table, scaled, preferred_element_type=jnp.float32
    ).astype(jnp.bfloat16)


def line_step(action, lines):
    parts, planes, rows, chunk = lines.shape
    groups = action.shape[0]
    lines = lines.reshape(parts * planes, groups, rows // groups, chunk)
    lines = lines.transpose(1, 0, 2, 3).reshape(groups, -1, chunk)
    lines = jnp.einsum(
        "gac,gcb->gab", action, lines, preferred_element_type=jnp.float32
    ).astype(jnp.bfloat16)
    lines = lines.reshape(groups, parts * planes, rows // groups, chunk).transpose(1, 0, 2, 3)
    return lines.reshape(parts, planes, rows, chunk)


def plane_back(backs, plane_table):
    side = NGRID * NGRID
    reals, imags = [], []
    for back in backs:
        chunk = back.shape[3]
        whole = [
            jnp.einsum(
                "qb,qk->bk",
                back[:, p].reshape(2 * side, chunk),
                plane_table,
                preferred_element_type=jnp.float32,
            )
            for p in range(back.shape[1])
        ]
        reals.append(jnp.concatenate([w[:, :side] for w in whole], 1))
        imags.append(jnp.concatenate([w[:, side:] for w in whole], 1))
    return jnp.concatenate(reals, 0), jnp.concatenate(imags, 0)


def waves(oxygens, gvectors, profile):
    local_g = profile.shape[0]
    side = NGRID * NGRID
    if local_g % side:
        phases = jnp.einsum("ai,ag->ig", oxygens, gvectors, precision=highest)
        return profile * jnp.cos(phases), profile * jnp.sin(phases)
    spots = oxygens.T
    flat = spots[:, 1:2] * gvectors[1:2, :side] + spots[:, 2:3] * gvectors[2:3, :side]
    flat_cos, flat_sin = jnp.cos(flat), jnp.sin(flat)
    along = spots[:, 0:1] * gvectors[0:1, ::side]
    along_cos, along_sin = jnp.cos(along), jnp.sin(along)
    cosines, sines = [], []
    for p in range(local_g // side):
        c, s = along_cos[:, p : p + 1], along_sin[:, p : p + 1]
        cosines.append(c * flat_cos - s * flat_sin)
        sines.append(s * flat_cos + c * flat_sin)
    return profile * jnp.concatenate(cosines, 1), profile * jnp.concatenate(sines, 1)


def per_device(positions, weights, psi, vloc):
    near_forces = field_forces(positions)
    weight_float = weights.astype(jnp.float32)
    mixing = weight_float / jnp.sum(weight_float, axis=1, keepdims=True)
    centres = jnp.einsum("cj,jan->can", mixing, positions, precision=highest)
    parts = lax.axis_size("ga")
    near_oxygen = centres[0][:, 0::3]
    own_waters = near_oxygen.shape[1]
    everyone = lax.dynamic_update_slice(
        jnp.zeros((3, own_waters * parts), jnp.float32),
        near_oxygen,
        (0, lax.axis_index("ga") * own_waters),
    )
    side = NGRID * NGRID
    whole_planes = psi.shape[3] % side == 0 and side % parts == 0
    if whole_planes:
        plane_table = plane_rotation()
        pieces = plane_out(psi, parts, plane_table)
        pieces[-1], everyone = lax.optimization_barrier((pieces[-1], everyone))
        lines = [exchange(piece) for piece in pieces]
        action = line_action(vloc, parts)
    oxygens = lax.psum(everyone, "ga")
    bands = psi.shape[1]
    local_g = psi.shape[3]
    flat_index = lax.axis_index("ga") * local_g + jnp.arange(local_g, dtype=jnp.int32)
    gvectors = jnp.stack(
        [
            frequency(flat_index // (NGRID * NGRID), NGRID),
            frequency(flat_index // NGRID % NGRID, NGRID),
            frequency(flat_index % NGRID, NGRID),
        ]
    )
    square = jnp.sum(gvectors * gvectors, axis=0)
    profile = jnp.exp(-0.5 * width_square * square)
    kinetic = 0.5 * square
    wave_cos, wave_sin = waves(oxygens, gvectors, profile)
    table = jnp.concatenate(
        [jnp.concatenate([wave_cos, -wave_sin], 1), jnp.concatenate([wave_sin, wave_cos], 1)], 0
    ).astype(jnp.bfloat16)
    wavefunc = psi[0].reshape(bands, 2 * local_g)
    partial_proj = (inner(table, wavefunc) * (1.0 / GVECS)).reshape(2, WATERS, bands)
    share = lax.psum_scatter(partial_proj, "ga", scatter_dimension=1, tiled=True).astype(
        jnp.bfloat16
    )
    table_blocks = table.reshape(2 * WATERS, 2 * local_g)
    copies = jnp.broadcast_to(share[None], (parts,) + share.shape)
    if whole_planes:
        lines[-1], copies = lax.optimization_barrier((lines[-1], copies))
    all_proj = lax.all_to_all(copies, "ga", split_axis=0, concat_axis=0, tiled=True)
    if whole_planes:
        moved = [line_step(action, line) for line in lines]
        moved[0], all_proj = lax.optimization_barrier((moved[0], all_proj))
        backs = [exchange(piece) for piece in moved]
    all_proj = all_proj.transpose(1, 0, 2, 3).reshape(2 * WATERS, bands)
    nonlocal_term = jnp.einsum(
        "ib,ig->bg", all_proj, table_blocks, preferred_element_type=jnp.float32
    )
    crossed = jnp.dot(all_proj, wavefunc, preferred_element_type=jnp.float32)
    weighted_re = crossed[:WATERS, :local_g] + crossed[WATERS:, local_g:]
    weighted_im = crossed[:WATERS, local_g:] - crossed[WATERS:, :local_g]
    mixed_wave = wave_cos * weighted_im + wave_sin * weighted_re
    force_part = (
        2.0
        * occupation
        * nonlocal_strength
        / GVECS
        * jnp.einsum("ag,ig->ai", gvectors, mixed_wave, precision=highest)
    )
    oxygen_force = lax.psum_scatter(force_part, "ga", scatter_dimension=1, tiled=True)
    hydrogen_zero = jnp.zeros_like(oxygen_force)
    dft_forces = [jnp.stack([oxygen_force, hydrogen_zero, hydrogen_zero], axis=2).reshape(3, -1)]
    wave_float = psi[0].astype(jnp.float32)
    if whole_planes:
        potential = plane_back(backs, plane_table)
    else:
        potential = grid_sum(psi, vloc, parts)
    hamil_re = (
        kinetic * wave_float[:, 0]
        + potential[0]
        + nonlocal_strength * nonlocal_term[:, :local_g]
    )
    hamil_im = (
        kinetic * wave_float[:, 1]
        + potential[1]
        + nonlocal_strength * nonlocal_term[:, local_g:]
    )
    trial_re = (wave_float[:, 0] - step_size * hamil_re).astype(jnp.bfloat16)
    trial_im = (wave_float[:, 1] - step_size * hamil_im).astype(jnp.bfloat16)
    row = lax.broadcasted_iota(jnp.int32, (bands, bands), 0)
    column = lax.broadcasted_iota(jnp.int32, (bands, bands), 1)
    even = inner(trial_re, trial_re) + inner(trial_im, trial_im)
    odd = inner(trial_im, trial_re) - inner(trial_re, trial_im)
    packed = jnp.where(row <= column, even, odd) * (1.0 / GVECS)
    shares = lax.all_to_all(
        packed.reshape(parts, bands // parts, bands), "ga", split_axis=0, concat_axis=0, tiled=True
    )
    own_rows = lax.broadcasted_iota(jnp.int32, (bands // parts, bands), 0) + lax.axis_index(
        "ga"
    ) * (bands // parts)
    own_columns = lax.broadcasted_iota(jnp.int32, (bands // parts, bands), 1)
    mixed_rows = jnp.where(own_rows == own_columns, 1.5, 0.0) - 0.5 * jnp.sum(shares, axis=0)
    mixed = lax.all_gather(mixed_rows.astype(jnp.bfloat16), "ga", axis=0, tiled=True)
    turned = mixed.T
    mix_re = jnp.where(row <= column, mixed, turned)
    mix_im = jnp.where(row > column, mixed, jnp.where(row < column, -turned, jnp.zeros_like(turned)))
    both = jnp.concatenate([trial_re, trial_im], 0)
    new_re = jnp.dot(
        jnp.concatenate([mix_re, -mix_im], 1), both, preferred_element_type=jnp.float32
    ).astype(jnp.bfloat16)
    new_im = jnp.dot(
        jnp.concatenate([mix_im, mix_re], 1), both, preferred_element_type=jnp.float32
    ).astype(jnp.bfloat16)
    new_waves = [jnp.stack([new_re, new_im], 1)]
    contracted_force = jnp.einsum("cj,can->jan", mixing, jnp.stack(dft_forces), precision=highest)
    bead_forces = near_forces + BEADS / CBEADS * contracted_force
    return (jnp.stack(new_waves), bead_forces)


def solution(mesh):
    placed = (P("rep", None, "ga"), P(), P("rep", None, None, "ga"), P("rep", None))
    return jax.shard_map(
        per_device,
        mesh=mesh,
        in_specs=placed,
        out_specs=(P("rep", None, None, "ga"), P("rep", None, "ga")),
        check_vma=False,
    )
```

```python
import jax
import jax.numpy as jnp
import numpy as np
from jax import lax
from jax.sharding import PartitionSpec as P

BEADS = 32
CBEADS = 1
WATERS = 256
NGRID = 32
GVECS = 32768
CHUNKS = 2


box_length = 20.0
bond_stiff = 0.5
bond_rest = 1.8
spring_stiff = 2.0
width_square = 0.09
step_size = 0.02
nonlocal_strength = 250.0
occupation = 2.0
highest = lax.Precision.HIGHEST


def frequency(index, count):
    signed = jnp.where(index < count // 2, index, index - count)
    return signed.astype(jnp.float32) * (2.0 * jnp.pi / box_length)


def field_forces(positions):
    oxygen = positions[:, :, 0::3]
    toward_one = positions[:, :, 1::3] - oxygen
    toward_two = positions[:, :, 2::3] - oxygen

    def stretch(offset):
        length = jnp.sqrt(jnp.sum(offset * offset, axis=1, keepdims=True))
        return -bond_stiff * (length - bond_rest) * offset / length

    pull_one = stretch(toward_one)
    pull_two = stretch(toward_two)
    bonds = jnp.stack([-(pull_one + pull_two), pull_one, pull_two], axis=3).reshape(positions.shape)
    springs = 2.0 * positions - jnp.roll(positions, 1, axis=0) - jnp.roll(positions, -1, axis=0)
    return bonds - spring_stiff * springs


def inner(left_mat, right_mat):
    return lax.dot_general(
        left_mat, right_mat, (((1,), (1,)), ((), ())), preferred_element_type=jnp.float32
    )


def real_form(freq_index, group_index):
    product = freq_index[:, None] * freq_index[None, :] % NGRID
    angle = product.astype(jnp.float32) * (2.0 * jnp.pi / NGRID)
    same = (group_index[:, None] == group_index[None, :]).astype(jnp.float32)
    cosines = jnp.cos(angle) * same
    sines = jnp.sin(angle) * same
    return jnp.stack([jnp.stack([cosines, sines], 1), jnp.stack([-sines, cosines], 1)], 0)


def plane_table():
    index = jnp.arange(NGRID, dtype=jnp.int32)
    return real_form(index, jnp.zeros_like(index))


def block_table(length, within):
    index = jnp.arange(length, dtype=jnp.int32)
    if within:
        return real_form(index % NGRID, index // NGRID)
    return real_form(index // NGRID, index % NGRID)


def grid_sum(psi, vloc, parts):
    bands = psi.shape[1]
    local_g = psi.shape[3]
    x_table = plane_table()
    z_table = block_table(local_g, True)
    y_table = block_table(NGRID * NGRID, False)
    grid_potential = vloc[0].reshape(1, 1, NGRID, NGRID * NGRID)
    grouped_raw = psi[0].reshape(parts, bands // parts, 2, local_g)
    planes = lax.all_to_all(grouped_raw, "ga", split_axis=0, concat_axis=3, tiled=True)
    band_count = planes.shape[1]
    blocks_whole = planes.astype(jnp.float32).reshape(band_count, 2, NGRID**3 // local_g, local_g)
    along_z = jnp.einsum("mckp,cpdq->mdkq", blocks_whole, z_table, precision=highest) * (
        1.0 / NGRID
    )
    grid = along_z.reshape(band_count, 2, NGRID, NGRID * NGRID)
    grid = jnp.einsum("mcxr,cxdw->mdwr", grid, x_table, precision=highest) * (1.0 / NGRID)
    grid = jnp.einsum("mcxp,cpdq->mdxq", grid, y_table, precision=highest) * (1.0 / NGRID)
    grid = grid * grid_potential
    grid = jnp.einsum("mdxq,cpdq->mcxp", grid, y_table, precision=highest)
    grid = jnp.einsum("mdwr,cxdw->mcxr", grid, x_table, precision=highest)
    returning = grid.reshape(1, band_count, 2, NGRID**3)
    returned = lax.all_to_all(
        returning.astype(jnp.bfloat16), "ga", split_axis=3, concat_axis=0, tiled=True
    ).astype(returning.dtype)
    returned = returned.reshape(bands, 2, local_g)
    potential = jnp.einsum("bdq,cpdq->bcp", returned, z_table, precision=highest)
    return potential[:, 0], potential[:, 1]


def plane_rotation():
    small = np.arange(NGRID)
    angle = small[:, None] * small[None, :] % NGRID * (2.0 * np.pi / NGRID)
    side = NGRID * NGRID
    wave = np.kron(np.exp(1j * angle), np.exp(1j * angle))
    real, imag = np.real(wave), np.imag(wave)
    table = np.stack([np.stack([real, -imag], 1), np.stack([imag, real], 1)], 1)
    return jnp.asarray(table.reshape(2 * side, 2 * side).astype(np.float32), jnp.bfloat16)


def line_rotation(group):
    small = np.arange(NGRID)
    angle = small[:, None] * small[None, :] % NGRID * (2.0 * np.pi / NGRID)
    real, imag = np.cos(angle), np.sin(angle)
    form = np.stack([np.stack([real, -imag], 2), np.stack([imag, real], 2)], 1)
    same = np.eye(group)
    table = form[:, None, :, :, None, :] * same[None, :, None, None, :, None]
    size = 2 * NGRID * group
    return jnp.asarray(table.reshape(size, size).astype(np.float32), jnp.bfloat16)


def plane_out(psi, parts, plane_table, offset):
    bands = psi.shape[1]
    side = NGRID * NGRID
    planes = psi.shape[3] // side
    chunk = bands // CHUNKS
    pieces = []
    for first in range(0, bands, chunk):
        part = lax.dynamic_slice_in_dim(psi[0], first + offset, chunk, axis=0).reshape(chunk, 2, planes, side)
        part = part.transpose(2, 0, 1, 3).reshape(planes, chunk, 2 * side)
        pieces.append(
            jnp.stack(
                [
                    jnp.einsum(
                        "qk,bk->qb", plane_table, part[p], preferred_element_type=jnp.float32
                    )
                    .astype(jnp.bfloat16)
                    .reshape(parts, 2 * side // parts, chunk)
                    for p in range(planes)
                ],
                1,
            )
        )
    return pieces


def exchange(piece):
    return lax.all_to_all(piece, "ga", split_axis=0, concat_axis=0, tiled=True)


def line_action(vloc, parts):
    side = NGRID * NGRID
    points = side // parts
    group = min(8, points)
    groups = points // group
    line_table = line_rotation(group)
    start = lax.axis_index("ga") * points
    own = lax.dynamic_slice_in_dim(vloc[0].reshape(NGRID, side), start, points, axis=1)
    own = own.reshape(NGRID, groups, group).transpose(1, 0, 2) * (1.0 / (NGRID * side))
    own = jnp.broadcast_to(own[..., None], (groups, NGRID, group, 2)).reshape(groups, -1, 1)
    scaled = (own * line_table.astype(jnp.float32)).astype(jnp.bfloat16)
    return jnp.einsum(
        "ea,gec->gac", line_table, scaled, preferred_element_type=jnp.float32
    ).astype(jnp.bfloat16)


def line_step(action, lines):
    parts, planes, rows, chunk = lines.shape
    groups = action.shape[0]
    lines = lines.reshape(parts * planes, groups, rows // groups, chunk)
    lines = lines.transpose(1, 0, 2, 3).reshape(groups, -1, chunk)
    lines = jnp.einsum(
        "gac,gcb->gab", action, lines, preferred_element_type=jnp.float32
    ).astype(jnp.bfloat16)
    lines = lines.reshape(groups, parts * planes, rows // groups, chunk).transpose(1, 0, 2, 3)
    return lines.reshape(parts, planes, rows, chunk)


def plane_back(backs, plane_table):
    side = NGRID * NGRID
    reals, imags = [], []
    for back in backs:
        chunk = back.shape[3]
        whole = [
            jnp.einsum(
                "qb,qk->bk",
                back[:, p].reshape(2 * side, chunk),
                plane_table,
                preferred_element_type=jnp.float32,
            )
            for p in range(back.shape[1])
        ]
        reals.append(jnp.concatenate([w[:, :side] for w in whole], 1))
        imags.append(jnp.concatenate([w[:, side:] for w in whole], 1))
    return jnp.concatenate(reals, 0), jnp.concatenate(imags, 0)


def waves(oxygens, gvectors, profile):
    local_g = profile.shape[0]
    side = NGRID * NGRID
    if local_g % side:
        phases = jnp.einsum("ai,ag->ig", oxygens, gvectors, precision=highest)
        return profile * jnp.cos(phases), profile * jnp.sin(phases)
    spots = oxygens.T
    flat = spots[:, 1:2] * gvectors[1:2, :side] + spots[:, 2:3] * gvectors[2:3, :side]
    flat_cos, flat_sin = jnp.cos(flat), jnp.sin(flat)
    along = spots[:, 0:1] * gvectors[0:1, ::side]
    along_cos, along_sin = jnp.cos(along), jnp.sin(along)
    cosines, sines = [], []
    for p in range(local_g // side):
        c, s = along_cos[:, p : p + 1], along_sin[:, p : p + 1]
        cosines.append(c * flat_cos - s * flat_sin)
        sines.append(s * flat_cos + c * flat_sin)
    return profile * jnp.concatenate(cosines, 1), profile * jnp.concatenate(sines, 1)


def per_device(positions, weights, psi, vloc):
    near_forces = field_forces(positions)
    weight_float = weights.astype(jnp.float32)
    mixing = weight_float / jnp.sum(weight_float, axis=1, keepdims=True)
    centres = jnp.einsum("cj,jan->can", mixing, positions, precision=highest)
    parts = lax.axis_size("ga")
    near_oxygen = centres[0][:, 0::3]
    own_waters = near_oxygen.shape[1]
    everyone = lax.dynamic_update_slice(
        jnp.zeros((3, own_waters * parts), jnp.float32),
        near_oxygen,
        (0, lax.axis_index("ga") * own_waters),
    )
    oxygens = lax.psum(everyone, "ga")
    side = NGRID * NGRID
    whole_planes = psi.shape[3] % side == 0 and side % parts == 0
    if whole_planes:
        plane_table = plane_rotation()
        pieces = plane_out(psi, parts, plane_table, (oxygens[0, 0] * 0.0).astype(jnp.int32))
        lines = [exchange(piece) for piece in pieces]
        action = line_action(vloc, parts)
    bands = psi.shape[1]
    local_g = psi.shape[3]
    flat_index = lax.axis_index("ga") * local_g + jnp.arange(local_g, dtype=jnp.int32)
    gvectors = jnp.stack(
        [
            frequency(flat_index // (NGRID * NGRID), NGRID),
            frequency(flat_index // NGRID % NGRID, NGRID),
            frequency(flat_index % NGRID, NGRID),
        ]
    )
    square = jnp.sum(gvectors * gvectors, axis=0)
    profile = jnp.exp(-0.5 * width_square * square)
    kinetic = 0.5 * square
    wave_cos, wave_sin = waves(oxygens, gvectors, profile)
    table = jnp.concatenate(
        [jnp.concatenate([wave_cos, -wave_sin], 1), jnp.concatenate([wave_sin, wave_cos], 1)], 0
    ).astype(jnp.bfloat16)
    wavefunc = psi[0].reshape(bands, 2 * local_g)
    partial_proj = (inner(table, wavefunc) * (1.0 / GVECS)).reshape(2, WATERS, bands)
    share = lax.psum_scatter(partial_proj, "ga", scatter_dimension=1, tiled=True).astype(
        jnp.bfloat16
    )
    table_blocks = table.reshape(2 * WATERS, 2 * local_g)
    copies = jnp.broadcast_to(share[None], (parts,) + share.shape)
    if whole_planes:
        lines[-1], copies = lax.optimization_barrier((lines[-1], copies))
    all_proj = lax.all_to_all(copies, "ga", split_axis=0, concat_axis=0, tiled=True)
    if whole_planes:
        moved = [line_step(action, line) for line in lines]
        moved[0], all_proj = lax.optimization_barrier((moved[0], all_proj))
        backs = [exchange(piece) for piece in moved]
    all_proj = all_proj.transpose(1, 0, 2, 3).reshape(2 * WATERS, bands)
    nonlocal_term = jnp.einsum(
        "ib,ig->bg", all_proj, table_blocks, preferred_element_type=jnp.float32
    )
    crossed = jnp.dot(all_proj, wavefunc, preferred_element_type=jnp.float32)
    weighted_re = crossed[:WATERS, :local_g] + crossed[WATERS:, local_g:]
    weighted_im = crossed[:WATERS, local_g:] - crossed[WATERS:, :local_g]
    mixed_wave = wave_cos * weighted_im + wave_sin * weighted_re
    force_part = (
        2.0
        * occupation
        * nonlocal_strength
        / GVECS
        * jnp.einsum("ag,ig->ai", gvectors, mixed_wave, precision=highest)
    )
    force_rows = force_part.reshape(3, parts, own_waters).transpose(1, 0, 2)
    force_rows = force_rows.reshape(parts, 1, 3 * own_waters)
    force_rows = jnp.pad(force_rows, ((0, 0), (0, 0), (0, bands - 3 * own_waters)))
    wave_float = psi[0].astype(jnp.float32)
    if whole_planes:
        potential = plane_back(backs, plane_table)
    else:
        potential = grid_sum(psi, vloc, parts)
    hamil_re = (
        kinetic * wave_float[:, 0]
        + potential[0]
        + nonlocal_strength * nonlocal_term[:, :local_g]
    )
    hamil_im = (
        kinetic * wave_float[:, 1]
        + potential[1]
        + nonlocal_strength * nonlocal_term[:, local_g:]
    )
    trial_re = (wave_float[:, 0] - step_size * hamil_re).astype(jnp.bfloat16)
    trial_im = (wave_float[:, 1] - step_size * hamil_im).astype(jnp.bfloat16)
    row = lax.broadcasted_iota(jnp.int32, (bands, bands), 0)
    column = lax.broadcasted_iota(jnp.int32, (bands, bands), 1)
    even = inner(trial_re, trial_re) + inner(trial_im, trial_im)
    odd = inner(trial_im, trial_re) - inner(trial_re, trial_im)
    packed = jnp.where(row <= column, even, odd) * (1.0 / GVECS)
    shares = lax.all_to_all(
        jnp.concatenate([packed.reshape(parts, bands // parts, bands), force_rows], 1),
        "ga",
        split_axis=0,
        concat_axis=0,
        tiled=True,
    )
    sums = jnp.sum(shares, axis=0)
    oxygen_force = sums[-1, : 3 * own_waters].reshape(3, own_waters)
    hydrogen_zero = jnp.zeros_like(oxygen_force)
    dft_forces = [jnp.stack([oxygen_force, hydrogen_zero, hydrogen_zero], axis=2).reshape(3, -1)]
    own_rows = lax.broadcasted_iota(jnp.int32, (bands // parts, bands), 0) + lax.axis_index(
        "ga"
    ) * (bands // parts)
    own_columns = lax.broadcasted_iota(jnp.int32, (bands // parts, bands), 1)
    mixed_rows = jnp.where(own_rows == own_columns, 1.5, 0.0) - 0.5 * sums[:-1]
    mixed = lax.all_gather(mixed_rows.astype(jnp.bfloat16), "ga", axis=0, tiled=True)
    turned = mixed.T
    mix_re = jnp.where(row <= column, mixed, turned)
    mix_im = jnp.where(row > column, mixed, jnp.where(row < column, -turned, jnp.zeros_like(turned)))
    both = jnp.concatenate([trial_re, trial_im], 0)
    new_re = jnp.dot(
        jnp.concatenate([mix_re, -mix_im], 1), both, preferred_element_type=jnp.float32
    ).astype(jnp.bfloat16)
    new_im = jnp.dot(
        jnp.concatenate([mix_im, mix_re], 1), both, preferred_element_type=jnp.float32
    ).astype(jnp.bfloat16)
    new_waves = [jnp.stack([new_re, new_im], 1)]
    contracted_force = jnp.einsum("cj,can->jan", mixing, jnp.stack(dft_forces), precision=highest)
    bead_forces = near_forces + BEADS / CBEADS * contracted_force
    return (jnp.stack(new_waves), bead_forces)


def solution(mesh):
    placed = (P("rep", None, "ga"), P(), P("rep", None, None, "ga"), P("rep", None))
    return jax.shard_map(
        per_device,
        mesh=mesh,
        in_specs=placed,
        out_specs=(P("rep", None, None, "ga"), P("rep", None, "ga")),
        check_vma=False,
    )
```
